32 devices in a mesh: ch: 4 (over z), ha: 2 (over x), dp: 4 (over y, core).
Axes of the slice: x: 2, y: 2, z: 4, core: 2. Of those that a mesh axis runs over, the one named last changes fastest.
Arguments:
- features: bfloat16 [384, 4, 4, 4, 128], P('ch', 'dp', None, 'ha'), may hold values from -26 to 26
- frame_count: int32 [4], P('dp'), may hold values from 1 to 4, as said below
- norm1_gain: float32 [384], P('ch'), may hold values from 0.5 to 2
- norm1_shift: float32 [384], P('ch'), may hold values from -3 to 3
- qkv_weight: bfloat16 [384, 1152], replicated, may hold values from -0.51031036 to 0.51031036
- qkv_bias: float32 [1152], replicated, may hold values from -3 to 3
- out_weight: bfloat16 [384, 384], replicated, may hold values from -0.3125 to 0.3125
- out_bias: float32 [384], replicated, may hold values from -3 to 3
- norm2_gain: float32 [384], P('ch'), may hold values from 0.5 to 2
- norm2_shift: float32 [384], P('ch'), may hold values from -3 to 3
- conv_weight: bfloat16 [3, 3, 3, 384, 384], P(None, None, None, 'ch'), may hold values from -0.0625 to 0.0625
- conv_bias: float32 [384], P('ch'), may hold values from -3 to 3
- cotangent: bfloat16 [384, 4, 4, 4, 128], P('ch', 'dp', None, 'ha'), may hold values from -0.0625 to 0.0625
Outputs:
- mixed: bfloat16 [384, 4, 4, 4, 128], P('ch', 'dp', None, 'ha')
- weight_grad: float32 [3, 3, 3, 384, 384], P(None, None, None, 'ch')
The draws below stay inside these ranges and needn't reach their ends.
Inputs may be any that keep to these rules, and one draw needn't show every extreme that they name: `frame_count`: some clip has all 4 frames valid and some clip only one.
All inputs are finite; a program needn't handle non-finite values.
Results may differ from the reference program's by a relative error of at most 0.015.
Values may be sent and summed in bfloat16 or wider, within the bound.
A program may use at most 64 MiB of HBM per device.

```python
import math
import jax
import jax.numpy as jnp
from jax import lax

C = 384
GROUPS = 32
FR = 4
W = 128
CLIPS = 4
HEIGHT = 4


def draw_features(key, part):
    first = jax.random.fold_in(jax.random.fold_in(key, 11), 0)
    shape = (C, CLIPS, FR, HEIGHT, W)
    height_pos = lax.broadcasted_iota(jnp.float32, shape, 3) / (HEIGHT - 1)
    ramp = 1.0 + 2.0 * height_pos
    return (jnp.clip(jax.random.normal(first, shape, jnp.float32), -5.0, 5.0) * ramp).astype(jnp.bfloat16)


def draw_frame_count(key, part):
    first, second = jax.random.split(jax.random.fold_in(key, 23))
    counts = jax.random.randint(first, (CLIPS,), 1, FR + 1)
    chosen = jax.random.randint(second, (), 0, CLIPS)
    other = (chosen + 1) % CLIPS
    places = jnp.arange(CLIPS)
    counts = jnp.where(places == chosen, FR, counts)
    counts = jnp.where(places == other, 1, counts)
    return counts.astype(jnp.int32)


def draw_qkv_weight(key, part):
    first, second, third = jax.random.split(jax.random.fold_in(key, 37), 3)
    query_w = jnp.clip(jax.random.normal(first, (C, C), jnp.float32), -5.0, 5.0) * (1.6 * C ** (-0.5))
    noise = jnp.clip(jax.random.normal(second, (C, C), jnp.float32), -5.0, 5.0)
    key_w = noise * (1.6 * C ** (-0.5))
    value_w = jnp.clip(jax.random.normal(third, (C, C), jnp.float32), -5.0, 5.0) * C ** (-0.5)
    return jnp.concatenate([query_w, key_w, value_w], axis=1).astype(jnp.bfloat16)


def shard_levels(rng, dims, pieces, least, largest):
    loudness, own = 1.0, jax.random.fold_in(rng, 6)
    for axis_at, blocks in pieces:
        draws = jnp.exp(jax.random.uniform(jax.random.fold_in(own, axis_at), (blocks,), jnp.float32, least / len(pieces), largest / len(pieces)))
        loudness = loudness * jnp.repeat(draws, dims[axis_at] // blocks).reshape([-1 if axis == axis_at else 1 for axis in range(len(dims))])
    return loudness


def gaussian(key, extent, width, most, cuts=(), dtype=jnp.bfloat16):
    drawn = jax.random.normal(key, extent, jnp.float32) * width
    if len(cuts) > 0:
        drawn = shard_levels(key, extent, cuts, -0.22, 0.18) * drawn
    return jnp.clip(drawn, min=-most, max=most).astype(dtype)


def setup_inputs(seed: int = 0) -> dict:
    seeds = jax.random.split(jax.random.key(seed), 14)
    features = draw_features(jax.random.fold_in(seeds[13], 71), 0)
    frame_count = draw_frame_count(jax.random.fold_in(seeds[13], 71), 0)
    norm1_gain = jnp.clip(jnp.exp(math.log(2.0) - 1.3862944 * jax.random.uniform(seeds[2], (C,), jnp.float32) ** shard_levels(seeds[2], (C,), ((0, 4),), -0.2, 0.2)), 0.5, 2.0)
    norm1_shift = gaussian(seeds[3], (C,), 0.5, 3.0, ((0, 4),), jnp.float32)
    qkv_weight = draw_qkv_weight(jax.random.fold_in(seeds[13], 71), 0)
    qkv_bias = gaussian(seeds[5], (3 * C,), 0.5, 3.0, (), jnp.float32)
    out_weight = gaussian(seeds[6], (C, C), C ** -0.5, 0.3125)
    out_bias = gaussian(seeds[7], (C,), 0.3, 3.0, (), jnp.float32)
    norm2_gain = jnp.clip(jnp.exp(math.log(2.0) - 1.3862944 * jax.random.uniform(seeds[8], (C,), jnp.float32) ** shard_levels(seeds[8], (C,), ((0, 4),), -0.2, 0.2)), 0.5, 2.0)
    norm2_shift = gaussian(seeds[9], (C,), 0.5, 3.0, ((0, 4),), jnp.float32)
    conv_weight = gaussian(seeds[10], (3, 3, 3, C, C), (27 * C) ** -0.5, 0.0625, ((3, 4),))
    conv_bias = gaussian(seeds[11], (C,), 0.3, 3.0, ((0, 4),), jnp.float32)
    cotangent = gaussian(seeds[12], (C, CLIPS, FR, HEIGHT, W), ((CLIPS * FR * HEIGHT * W) ** -0.5), 0.0625, ((0, 4), (1, 4), (3, 2)))
    return dict(features=features, frame_count=frame_count, norm1_gain=norm1_gain, norm1_shift=norm1_shift, qkv_weight=qkv_weight, qkv_bias=qkv_bias, out_weight=out_weight, out_bias=out_bias, norm2_gain=norm2_gain, norm2_shift=norm2_shift, conv_weight=conv_weight, conv_bias=conv_bias, cotangent=cotangent)


EPS = 1e-06

def frame_mask(frame_count):
    position = lax.broadcasted_iota(jnp.int32, (frame_count.shape[0], FR), 1)
    return (position < frame_count[:, None].astype(jnp.int32)).astype(jnp.float32)

def group_norm(values, mask, count, gain, shift):
    data = values.astype(jnp.float32).reshape(GROUPS, C // GROUPS, CLIPS, FR, HEIGHT * W)
    first = jnp.einsum('gkbfp,bf->gb', data, mask)
    second = jnp.einsum('gkbfp,bf->gb', data * data, mask)
    mean = first / count[None, :]
    var = second / count[None, :] - mean * mean
    scale = lax.rsqrt(var + EPS)
    normed = (data - mean[:, None, :, None, None]) * scale[:, None, :, None, None]
    normed = normed.reshape(C, CLIPS, FR, HEIGHT, W)
    return normed * gain[:, None, None, None, None] + shift[:, None, None, None, None]

def reference(features, frame_count, norm1_gain, norm1_shift, qkv_weight, qkv_bias, out_weight, out_bias, norm2_gain, norm2_shift, conv_weight, conv_bias, cotangent):
    mask = frame_mask(frame_count)
    count = frame_count.astype(jnp.float32) * (C // GROUPS * HEIGHT * W)
    normed = group_norm(features, mask, count, norm1_gain, norm1_shift).astype(jnp.bfloat16)
    frame_tokens = HEIGHT * W
    block_rows = math.gcd(frame_tokens, 1024)
    items = jnp.moveaxis(normed.reshape(C, CLIPS * FR, frame_tokens), 1, 0)
    qkv_full = qkv_weight.astype(jnp.float32)

    def attend_frame(item):
        proj = jnp.dot(item.T.astype(jnp.float32), qkv_full, preferred_element_type=jnp.float32) + qkv_bias
        proj = proj.astype(jnp.bfloat16)
        queries = proj[:, :C]
        keys = proj[:, C:2 * C].astype(jnp.float32)
        values = proj[:, 2 * C:].astype(jnp.float32)

        def one_block(query):
            scores = jnp.dot(query.astype(jnp.float32), keys.T, preferred_element_type=jnp.float32) * C ** (-0.5)
            top = lax.optimization_barrier(jnp.max(scores, axis=1, keepdims=True))
            weights = jnp.exp(scores - top)
            total = lax.optimization_barrier(jnp.sum(weights, axis=1, keepdims=True))
            rounded = lax.optimization_barrier(weights.astype(jnp.bfloat16))
            out = jnp.dot(rounded.astype(jnp.float32), values, preferred_element_type=jnp.float32) / total
            return out.astype(jnp.bfloat16)
        blocks = lax.map(one_block, queries.reshape(frame_tokens // block_rows, block_rows, C))
        return blocks.reshape(frame_tokens, C)
    attended = lax.map(attend_frame, items)
    update = lax.dot_general(out_weight.astype(jnp.float32), attended.astype(jnp.float32), (((0,), (2,)), ((), ())), preferred_element_type=jnp.float32)
    update = (update + out_bias[:, None, None]).astype(jnp.bfloat16).reshape(C, CLIPS, FR, HEIGHT, W)
    hidden = (features.astype(jnp.float32) + update.astype(jnp.float32)).astype(jnp.bfloat16)
    gated = jax.nn.silu(group_norm(hidden, mask, count, norm2_gain, norm2_shift)).astype(jnp.bfloat16)
    padded = jnp.pad(gated.astype(jnp.float32), ((0, 0), (0, 0), (2, 0), (1, 1), (1, 1)))
    masked_cot = (cotangent * mask.astype(jnp.bfloat16)[None, :, :, None, None]).astype(jnp.float32)
    conv = jnp.zeros((C, CLIPS, FR, HEIGHT, W), jnp.float32)
    grads = []
    for kt in range(3):
        for ky in range(3):
            for kx in range(3):
                window = padded[:, :, kt:kt + FR, ky:ky + HEIGHT, kx:kx + W]
                conv = conv + lax.dot_general(conv_weight[kt, ky, kx].astype(jnp.float32), window, (((0,), (0,)), ((), ())), preferred_element_type=jnp.float32)
                grads.append(lax.dot_general(window, masked_cot, (((1, 2, 3, 4), (1, 2, 3, 4)), ((), ())), preferred_element_type=jnp.float32))
    weight_grad = jnp.stack(grads).reshape(3, 3, 3, C, C)
    mixed = mask[None, :, :, None, None] * (hidden.astype(jnp.float32) + conv + conv_bias[:, None, None, None, None])
    return (mixed.astype(jnp.bfloat16), weight_grad)
```

```python
import jax
import jax.numpy as jnp
from jax import lax
from jax.sharding import PartitionSpec as P

GROUPS = 32


EPS = 1e-06


def padded_2(x, sides, width):
    for axis, dim in sides:
        count, length = (lax.axis_size(axis), x.shape[dim])
        up = [(i, (i + 1) % count) for i in range(count - 1)]
        down = [(j, i) for i, j in up]
        last = lax.slice_in_dim(x, length - width, length, axis=dim)
        leading = lax.slice_in_dim(x, 0, width, axis=dim)
        before = lax.ppermute(last, axis, up)
        after = lax.ppermute(leading, axis, down)
        x = jnp.concatenate([before, x, after], axis=dim)
    return x


def frame_mask(frame_count, frames):
    position = lax.broadcasted_iota(jnp.int32, (frame_count.shape[0], frames), 1)
    return (position < frame_count[:, None]).astype(jnp.float32)


def moments(values, mask, groups):
    chans, clips, frames, rows, cols = values.shape
    data = values.astype(jnp.float32).reshape(groups, chans // groups, clips, frames, rows * cols)
    first = jnp.einsum("gkbfp,bf->gb", data, mask)
    second = jnp.einsum("gkbfp,bf->gb", data * data, mask)
    return (first, second)


def normalize(values, first, second, count, gain, shift, groups):
    chans, clips, frames, rows, cols = values.shape
    mean = first / count[None, :]
    var = second / count[None, :] - mean * mean
    scale = lax.rsqrt(var + EPS)
    data = values.astype(jnp.float32).reshape(groups, chans // groups, clips, frames, rows * cols)
    normed = (data - mean[:, None, :, None, None]) * scale[:, None, :, None, None]
    normed = normed.reshape(values.shape)
    return normed * gain[:, None, None, None, None] + shift[:, None, None, None, None]


def attend(carry, queries, keys, values, scale):
    top, total, acc = carry
    scores = jnp.einsum("itc,isc->its", queries, keys, preferred_element_type=jnp.float32) * scale
    new_top = jnp.max(scores, axis=2)
    factor = jnp.exp(top - new_top)
    weights = jnp.exp(scores - new_top[..., None])
    total = total * factor + jnp.sum(weights, axis=2)
    acc = acc * factor[..., None] + jnp.einsum(
        "its,isc->itc", weights.astype(jnp.bfloat16), values, preferred_element_type=jnp.float32
    )
    return (new_top, total, acc)


def tap_stack(padded, time_tap, frames, rows, cols):
    windows = []
    for row_tap in range(3):
        for col_tap in range(3):
            windows.append(
                padded[
                    :,
                    :,
                    time_tap : time_tap + frames,
                    row_tap : row_tap + rows,
                    col_tap : col_tap + cols,
                ]
            )
    return jnp.concatenate(windows, axis=0)


def body(
    features,
    frame_count,
    norm1_gain,
    norm1_shift,
    qkv_weight,
    qkv_bias,
    out_weight,
    out_bias,
    norm2_gain,
    norm2_shift,
    conv_weight,
    conv_bias,
    cotangent,
):
    chans, clips, frames, rows, cols = features.shape
    groups = GROUPS // lax.axis_size("ch")
    mask = frame_mask(frame_count, frames)
    count = frame_count.astype(jnp.float32) * (chans // groups * rows * lax.axis_size("ha") * cols)
    first, second = moments(features, mask, groups)
    first, second = lax.psum((first, second), "ha")
    normed = normalize(features, first, second, count, norm1_gain, norm1_shift, groups).astype(
        jnp.bfloat16
    )
    by_frame = lax.all_to_all(normed, "ch", split_axis=2, concat_axis=0, tiled=True)
    width = by_frame.shape[0]
    items = clips * by_frame.shape[2]
    tok_rows = rows * cols
    tokens = by_frame.reshape(width, items, tok_rows)
    queries = lax.dot_general(
        tokens, qkv_weight[:, :width], (((0,), (0,)), ((), ())), preferred_element_type=jnp.float32
    )
    queries = (queries + qkv_bias[:width]).astype(jnp.bfloat16)
    scale = width ** (-0.5)
    start_carry = (
        jnp.full((items, tok_rows), -jnp.inf, jnp.float32),
        jnp.zeros((items, tok_rows), jnp.float32),
        jnp.zeros((items, tok_rows, width), jnp.float32),
    )
    pairs = lax.dot_general(
        tokens, qkv_weight[:, width:], (((0,), (0,)), ((), ())), preferred_element_type=jnp.float32
    )
    pairs = (pairs + qkv_bias[width:]).astype(jnp.bfloat16)
    piece = lax.all_gather(pairs, "ha", axis=1, tiled=True)
    top, total, acc = attend(start_carry, queries, piece[..., :width], piece[..., width:], scale)
    attended = (acc / total[..., None]).astype(jnp.bfloat16)
    projected = lax.dot_general(
        out_weight, attended, (((0,), (2,)), ((), ())), preferred_element_type=jnp.float32
    )
    projected = (projected + out_bias[:, None, None]).astype(jnp.bfloat16).reshape(by_frame.shape)
    update = lax.all_to_all(projected, "ch", split_axis=0, concat_axis=2, tiled=True)
    hidden = (features.astype(jnp.float32) + update.astype(jnp.float32)).astype(jnp.bfloat16)
    first, second = moments(hidden, mask, groups)
    first, second = lax.psum((first, second), "ha")
    gated = jax.nn.silu(
        normalize(hidden, first, second, count, norm2_gain, norm2_shift, groups)
    ).astype(jnp.bfloat16)
    with_rows = padded_2(gated, (("ha", 3),), 1)
    padded = jnp.pad(with_rows, ((0, 0), (0, 0), (2, 0), (0, 0), (1, 1)))
    stacks = [tap_stack(padded, time_tap, frames, rows, cols) for time_tap in range(3)]
    amount = chans * lax.axis_size("ch")
    summed = jnp.zeros((amount, clips, frames, rows, cols), jnp.float32)
    for time_tap in range(3):
        part = conv_weight[time_tap].reshape(9 * chans, amount)
        summed = summed + lax.dot_general(
            part, stacks[time_tap], (((0,), (0,)), ((), ())), preferred_element_type=jnp.float32
        )
    conv_out = lax.psum_scatter(
        summed.astype(jnp.bfloat16), "ch", scatter_dimension=0, tiled=True
    ).astype(jnp.float32)
    mixed = mask[None, :, :, None, None] * (
        hidden.astype(jnp.float32) + conv_out + conv_bias[:, None, None, None, None]
    )
    mixed = mixed.astype(jnp.bfloat16)
    masked_cot = cotangent * mask.astype(jnp.bfloat16)[None, :, :, None, None]
    full_width = chans * lax.axis_size("ch")
    carry = jnp.zeros((3, 9 * chans, full_width), jnp.float32)
    piece = lax.all_gather(masked_cot, "ch", axis=0, tiled=True)
    start = jnp.int32(0)
    for time_tap in range(3):
        part = lax.dot_general(
            stacks[time_tap],
            piece,
            (((1, 2, 3, 4), (1, 2, 3, 4)), ((), ())),
            preferred_element_type=jnp.float32,
        )
        carry = lax.dynamic_update_slice(
            carry, part[None], (jnp.int32(time_tap), jnp.int32(0), start)
        )
    grad_table = carry
    grad_table = grad_table.reshape(3, 3, 3, chans, full_width)
    weight_grad = lax.psum(grad_table.astype(jnp.bfloat16), ("ha", "dp")).astype(jnp.float32)
    return (mixed, weight_grad)


def solution(mesh):
    placed = (
        P("ch", "dp", None, "ha", None),
        P("dp"),
        P("ch"),
        P("ch"),
        P(),
        P(),
        P(),
        P(),
        P("ch"),
        P("ch"),
        P(None, None, None, "ch", None),
        P("ch"),
        P("ch", "dp", None, "ha", None),
    )
    return jax.shard_map(
        body,
        mesh=mesh,
        in_specs=placed,
        out_specs=(P("ch", "dp", None, "ha", None), P(None, None, None, "ch", None)),
        check_vma=False,
    )
```

```python
import jax
import jax.numpy as jnp
from jax import lax
from jax.sharding import PartitionSpec as P

GROUPS = 32


EPS = 1e-06


def padded_2(x, sides, width):
    for axis, dim in sides:
        count, length = (lax.axis_size(axis), x.shape[dim])
        up = [(i, (i + 1) % count) for i in range(count - 1)]
        down = [(j, i) for i, j in up]
        last = lax.slice_in_dim(x, length - width, length, axis=dim)
        leading = lax.slice_in_dim(x, 0, width, axis=dim)
        before = lax.ppermute(last, axis, up)
        after = lax.ppermute(leading, axis, down)
        x = jnp.concatenate([before, x, after], axis=dim)
    return x


def frame_mask(frame_count, frames):
    position = lax.broadcasted_iota(jnp.int32, (frame_count.shape[0], frames), 1)
    return (position < frame_count[:, None]).astype(jnp.float32)


def moments(values, mask, groups):
    chans, clips, frames, rows, cols = values.shape
    data = values.astype(jnp.float32).reshape(groups, chans // groups, clips, frames, rows * cols)
    first = jnp.einsum("gkbfp,bf->gb", data, mask)
    second = jnp.einsum("gkbfp,bf->gb", data * data, mask)
    return (first, second)


def normalize(values, first, second, count, gain, shift, groups):
    chans, clips, frames, rows, cols = values.shape
    mean = first / count[None, :]
    var = second / count[None, :] - mean * mean
    scale = lax.rsqrt(var + EPS)
    data = values.astype(jnp.float32).reshape(groups, chans // groups, clips, frames, rows * cols)
    normed = (data - mean[:, None, :, None, None]) * scale[:, None, :, None, None]
    normed = normed.reshape(values.shape)
    return normed * gain[:, None, None, None, None] + shift[:, None, None, None, None]


def attend(carry, queries, keys, values, scale):
    top, total, acc = carry
    scores = jnp.einsum("itc,isc->its", queries, keys, preferred_element_type=jnp.float32) * scale
    new_top = jnp.max(scores, axis=2)
    factor = jnp.exp(top - new_top)
    weights = jnp.exp(scores - new_top[..., None])
    total = total * factor + jnp.sum(weights, axis=2)
    acc = acc * factor[..., None] + jnp.einsum(
        "its,isc->itc", weights.astype(jnp.bfloat16), values, preferred_element_type=jnp.float32
    )
    return (new_top, total, acc)


def tap_stack(padded, time_tap, frames, rows, cols):
    windows = []
    for row_tap in range(3):
        for col_tap in range(3):
            windows.append(
                padded[
                    :,
                    :,
                    time_tap : time_tap + frames,
                    row_tap : row_tap + rows,
                    col_tap : col_tap + cols,
                ]
            )
    return jnp.concatenate(windows, axis=0)


def butterfly_sum(table, axes):
    steps = []
    for axis in axes:
        size = lax.axis_size(axis)
        for bit in range(size.bit_length() - 1):
            steps.append((axis, bit, size))
    length = table.shape[0]
    unit = (1 << len(steps)) * 8
    padded = -(-length // unit) * unit
    work = jnp.pad(table, ((0, padded - length), (0, 0)))
    for axis, bit, size in steps:
        side = (lax.axis_index(axis) >> bit) & 1
        halves = work.reshape(2, work.shape[0] // 2, work.shape[1])
        keep = lax.dynamic_index_in_dim(halves, side, keepdims=False)
        send = lax.dynamic_index_in_dim(halves, 1 - side, keepdims=False)
        perm = [(i, i ^ (1 << bit)) for i in range(size)]
        got = lax.ppermute(send.astype(jnp.bfloat16), axis, perm)
        work = keep + got.astype(jnp.float32)
    work = work.astype(jnp.bfloat16)
    for axis, bit, size in reversed(steps):
        side = (lax.axis_index(axis) >> bit) & 1
        perm = [(i, i ^ (1 << bit)) for i in range(size)]
        got = lax.ppermute(work, axis, perm)
        pair = jnp.stack([work, got])
        first = lax.dynamic_index_in_dim(pair, side, keepdims=False)
        second = lax.dynamic_index_in_dim(pair, 1 - side, keepdims=False)
        work = jnp.concatenate([first, second], axis=0)
    return work[:length].astype(jnp.float32)


def body(
    features,
    frame_count,
    norm1_gain,
    norm1_shift,
    qkv_weight,
    qkv_bias,
    out_weight,
    out_bias,
    norm2_gain,
    norm2_shift,
    conv_weight,
    conv_bias,
    cotangent,
):
    chans, clips, frames, rows, cols = features.shape
    groups = GROUPS // lax.axis_size("ch")
    mask = frame_mask(frame_count, frames)
    count = frame_count.astype(jnp.float32) * (chans // groups * rows * lax.axis_size("ha") * cols)
    first, second = moments(features, mask, groups)
    first, second = lax.psum((first, second), "ha")
    normed = normalize(features, first, second, count, norm1_gain, norm1_shift, groups).astype(
        jnp.bfloat16
    )
    by_frame = lax.all_to_all(normed, "ch", split_axis=2, concat_axis=0, tiled=True)
    width = by_frame.shape[0]
    items = clips * by_frame.shape[2]
    tok_rows = rows * cols
    tokens = by_frame.reshape(width, items, tok_rows)
    queries = lax.dot_general(
        tokens, qkv_weight[:, :width], (((0,), (0,)), ((), ())), preferred_element_type=jnp.float32
    )
    queries = (queries + qkv_bias[:width]).astype(jnp.bfloat16)
    scale = width ** (-0.5)
    start_carry = (
        jnp.full((items, tok_rows), -jnp.inf, jnp.float32),
        jnp.zeros((items, tok_rows), jnp.float32),
        jnp.zeros((items, tok_rows, width), jnp.float32),
    )
    pairs = lax.dot_general(
        tokens, qkv_weight[:, width:], (((0,), (0,)), ((), ())), preferred_element_type=jnp.float32
    )
    pairs = (pairs + qkv_bias[width:]).astype(jnp.bfloat16)
    piece = lax.all_gather(pairs, "ha", axis=1, tiled=True)
    top, total, acc = attend(start_carry, queries, piece[..., :width], piece[..., width:], scale)
    attended = (acc / total[..., None]).astype(jnp.bfloat16)
    projected = lax.dot_general(
        out_weight, attended, (((0,), (2,)), ((), ())), preferred_element_type=jnp.float32
    )
    projected = (projected + out_bias[:, None, None]).astype(jnp.bfloat16).reshape(by_frame.shape)
    update = lax.all_to_all(projected, "ch", split_axis=0, concat_axis=2, tiled=True)
    hidden = (features.astype(jnp.float32) + update.astype(jnp.float32)).astype(jnp.bfloat16)
    first, second = moments(hidden, mask, groups)
    first, second = lax.psum((first, second), "ha")
    gated = jax.nn.silu(
        normalize(hidden, first, second, count, norm2_gain, norm2_shift, groups)
    ).astype(jnp.bfloat16)
    with_rows = padded_2(gated, (("ha", 3),), 1)
    padded = jnp.pad(with_rows, ((0, 0), (0, 0), (2, 0), (0, 0), (1, 1)))
    stacks = [tap_stack(padded, time_tap, frames, rows, cols) for time_tap in range(3)]
    amount = chans * lax.axis_size("ch")
    summed = jnp.zeros((amount, clips, frames, rows, cols), jnp.float32)
    for time_tap in range(3):
        part = conv_weight[time_tap].reshape(9 * chans, amount)
        summed = summed + lax.dot_general(
            part, stacks[time_tap], (((0,), (0,)), ((), ())), preferred_element_type=jnp.float32
        )
    conv_out = lax.psum_scatter(
        summed.astype(jnp.bfloat16), "ch", scatter_dimension=0, tiled=True
    ).astype(jnp.float32)
    mixed = mask[None, :, :, None, None] * (
        hidden.astype(jnp.float32) + conv_out + conv_bias[:, None, None, None, None]
    )
    mixed = mixed.astype(jnp.bfloat16)
    masked_cot = cotangent * mask.astype(jnp.bfloat16)[None, :, :, None, None]
    full_width = chans * lax.axis_size("ch")
    carry = jnp.zeros((3, 9 * chans, full_width), jnp.float32)
    piece = lax.all_gather(masked_cot, "ch", axis=0, tiled=True)
    start = jnp.int32(0)
    for time_tap in range(3):
        part = lax.dot_general(
            stacks[time_tap],
            piece,
            (((1, 2, 3, 4), (1, 2, 3, 4)), ((), ())),
            preferred_element_type=jnp.float32,
        )
        carry = lax.dynamic_update_slice(
            carry, part[None], (jnp.int32(time_tap), jnp.int32(0), start)
        )
    weight_grad = butterfly_sum(carry.reshape(27 * chans, full_width), ("dp", "ha"))
    weight_grad = weight_grad.reshape(3, 3, 3, chans, full_width)
    return (mixed, weight_grad)


def solution(mesh):
    placed = (
        P("ch", "dp", None, "ha", None),
        P("dp"),
        P("ch"),
        P("ch"),
        P(),
        P(),
        P(),
        P(),
        P("ch"),
        P("ch"),
        P(None, None, None, "ch", None),
        P("ch"),
        P("ch", "dp", None, "ha", None),
    )
    return jax.shard_map(
        body,
        mesh=mesh,
        in_specs=placed,
        out_specs=(P("ch", "dp", None, "ha", None), P(None, None, None, "ch", None)),
        check_vma=False,
    )
```

```python
import jax
import jax.numpy as jnp
from jax import lax
from jax.sharding import PartitionSpec as P

GROUPS = 32


EPS = 1e-06


def padded_2(x, sides, width):
    for axis, dim in sides:
        count, length = (lax.axis_size(axis), x.shape[dim])
        up = [(i, (i + 1) % count) for i in range(count - 1)]
        down = [(j, i) for i, j in up]
        last = lax.slice_in_dim(x, length - width, length, axis=dim)
        leading = lax.slice_in_dim(x, 0, width, axis=dim)
        before = lax.ppermute(last, axis, up)
        after = lax.ppermute(leading, axis, down)
        x = jnp.concatenate([before, x, after], axis=dim)
    return x


def frame_mask(frame_count, frames):
    position = lax.broadcasted_iota(jnp.int32, (frame_count.shape[0], frames), 1)
    return (position < frame_count[:, None]).astype(jnp.float32)


def moments(values, mask, groups):
    chans, clips, frames, rows, cols = values.shape
    data = values.astype(jnp.float32).reshape(groups, chans // groups, clips, frames, rows * cols)
    first = jnp.einsum("gkbfp,bf->gb", data, mask)
    second = jnp.einsum("gkbfp,bf->gb", data * data, mask)
    return (first, second)


def normalize(values, first, second, count, gain, shift, groups):
    chans, clips, frames, rows, cols = values.shape
    mean = first / count[None, :]
    var = second / count[None, :] - mean * mean
    scale = lax.rsqrt(var + EPS)
    data = values.astype(jnp.float32).reshape(groups, chans // groups, clips, frames, rows * cols)
    normed = (data - mean[:, None, :, None, None]) * scale[:, None, :, None, None]
    normed = normed.reshape(values.shape)
    return normed * gain[:, None, None, None, None] + shift[:, None, None, None, None]


def attend(carry, queries, keys, values, scale):
    top, total, acc = carry
    scores = jnp.einsum("itc,isc->its", queries, keys, preferred_element_type=jnp.float32) * scale
    new_top = jnp.max(scores, axis=2)
    factor = jnp.exp(top - new_top)
    weights = jnp.exp(scores - new_top[..., None])
    total = total * factor + jnp.sum(weights, axis=2)
    acc = acc * factor[..., None] + jnp.einsum(
        "its,isc->itc", weights.astype(jnp.bfloat16), values, preferred_element_type=jnp.float32
    )
    return (new_top, total, acc)


def tap_stack(padded, time_tap, frames, rows, cols):
    windows = []
    for row_tap in range(3):
        for col_tap in range(3):
            windows.append(
                padded[
                    :,
                    :,
                    time_tap : time_tap + frames,
                    row_tap : row_tap + rows,
                    col_tap : col_tap + cols,
                ]
            )
    return jnp.concatenate(windows, axis=0)


def butterfly_sum(table, axes):
    steps = []
    for axis in axes:
        size = lax.axis_size(axis)
        for bit in range(size.bit_length() - 1):
            steps.append((axis, bit, size))
    length = table.shape[0]
    unit = (1 << len(steps)) * 8
    padded = -(-length // unit) * unit
    work = jnp.pad(table, ((0, padded - length), (0, 0)))
    for axis, bit, size in steps:
        side = (lax.axis_index(axis) >> bit) & 1
        halves = work.reshape(2, work.shape[0] // 2, work.shape[1])
        keep = lax.dynamic_index_in_dim(halves, side, keepdims=False)
        send = lax.dynamic_index_in_dim(halves, 1 - side, keepdims=False)
        perm = [(i, i ^ (1 << bit)) for i in range(size)]
        got = lax.ppermute(send.astype(jnp.bfloat16), axis, perm)
        work = keep + got.astype(jnp.float32)
    work = work.astype(jnp.bfloat16)
    for axis, bit, size in reversed(steps):
        side = (lax.axis_index(axis) >> bit) & 1
        perm = [(i, i ^ (1 << bit)) for i in range(size)]
        got = lax.ppermute(work, axis, perm)
        pair = jnp.stack([work, got])
        first = lax.dynamic_index_in_dim(pair, side, keepdims=False)
        second = lax.dynamic_index_in_dim(pair, 1 - side, keepdims=False)
        work = jnp.concatenate([first, second], axis=0)
    return work[:length].astype(jnp.float32)


def body(
    features,
    frame_count,
    norm1_gain,
    norm1_shift,
    qkv_weight,
    qkv_bias,
    out_weight,
    out_bias,
    norm2_gain,
    norm2_shift,
    conv_weight,
    conv_bias,
    cotangent,
):
    chans, clips, frames, rows, cols = features.shape
    groups = GROUPS // lax.axis_size("ch")
    mask = frame_mask(frame_count, frames)
    count = frame_count.astype(jnp.float32) * (chans // groups * rows * lax.axis_size("ha") * cols)
    first, second = moments(features, mask, groups)
    first, second = lax.psum((first, second), "ha")
    normed = normalize(features, first, second, count, norm1_gain, norm1_shift, groups).astype(
        jnp.bfloat16
    )
    by_frame = lax.all_to_all(normed, "ch", split_axis=2, concat_axis=0, tiled=True)
    width = by_frame.shape[0]
    items = clips * by_frame.shape[2]
    tok_rows = rows * cols
    tokens = by_frame.reshape(width, items, tok_rows)
    queries = lax.dot_general(
        tokens, qkv_weight[:, :width], (((0,), (0,)), ((), ())), preferred_element_type=jnp.float32
    )
    queries = (queries + qkv_bias[:width]).astype(jnp.bfloat16)
    scale = width ** (-0.5)
    start_carry = (
        jnp.full((items, tok_rows), -jnp.inf, jnp.float32),
        jnp.zeros((items, tok_rows), jnp.float32),
        jnp.zeros((items, tok_rows, width), jnp.float32),
    )
    pairs = lax.dot_general(
        tokens, qkv_weight[:, width:], (((0,), (0,)), ((), ())), preferred_element_type=jnp.float32
    )
    pairs = (pairs + qkv_bias[width:]).astype(jnp.bfloat16)
    piece = lax.all_gather(pairs, "ha", axis=1, tiled=True)
    top, total, acc = attend(start_carry, queries, piece[..., :width], piece[..., width:], scale)
    attended = (acc / total[..., None]).astype(jnp.bfloat16)
    projected = lax.dot_general(
        out_weight, attended, (((0,), (2,)), ((), ())), preferred_element_type=jnp.float32
    )
    projected = (projected + out_bias[:, None, None]).astype(jnp.bfloat16).reshape(by_frame.shape)
    update = lax.all_to_all(projected, "ch", split_axis=0, concat_axis=2, tiled=True)
    hidden = (features.astype(jnp.float32) + update.astype(jnp.float32)).astype(jnp.bfloat16)
    first, second = moments(hidden, mask, groups)
    first, second = lax.psum((first, second), "ha")
    gated = jax.nn.silu(
        normalize(hidden, first, second, count, norm2_gain, norm2_shift, groups)
    ).astype(jnp.bfloat16)
    with_rows = padded_2(gated, (("ha", 3),), 1)
    padded = jnp.pad(with_rows, ((0, 0), (0, 0), (2, 0), (0, 0), (1, 1)))
    stacks = [tap_stack(padded, time_tap, frames, rows, cols) for time_tap in range(3)]
    amount = chans * lax.axis_size("ch")
    summed = jnp.zeros((amount, clips, frames, rows, cols), jnp.float32)
    for time_tap in range(3):
        part = conv_weight[time_tap].reshape(9 * chans, amount)
        summed = summed + lax.dot_general(
            part, stacks[time_tap], (((0,), (0,)), ((), ())), preferred_element_type=jnp.float32
        )
    summed, stacks = lax.optimization_barrier((summed.astype(jnp.bfloat16), stacks))
    shares = lax.axis_size("ch")
    parts = summed.reshape((shares, amount // shares) + summed.shape[1:])
    parts = lax.all_to_all(parts, "ch", split_axis=0, concat_axis=0, tiled=True)
    conv_out = jnp.sum(parts.astype(jnp.float32), axis=0)
    mixed = mask[None, :, :, None, None] * (
        hidden.astype(jnp.float32) + conv_out + conv_bias[:, None, None, None, None]
    )
    mixed = mixed.astype(jnp.bfloat16)
    masked_cot = cotangent * mask.astype(jnp.bfloat16)[None, :, :, None, None]
    full_width = chans * lax.axis_size("ch")
    carry = jnp.zeros((3, 9 * chans, full_width), jnp.float32)
    piece = lax.all_gather(masked_cot, "ch", axis=0, tiled=True)
    start = jnp.int32(0)
    for time_tap in range(3):
        part = lax.dot_general(
            stacks[time_tap],
            piece,
            (((1, 2, 3, 4), (1, 2, 3, 4)), ((), ())),
            preferred_element_type=jnp.float32,
        )
        carry = lax.dynamic_update_slice(
            carry, part[None], (jnp.int32(time_tap), jnp.int32(0), start)
        )
    weight_grad = butterfly_sum(carry.reshape(27 * chans, full_width), ("dp", "ha"))
    weight_grad = weight_grad.reshape(3, 3, 3, chans, full_width)
    return (mixed, weight_grad)


def solution(mesh):
    placed = (
        P("ch", "dp", None, "ha", None),
        P("dp"),
        P("ch"),
        P("ch"),
        P(),
        P(),
        P(),
        P(),
        P("ch"),
        P("ch"),
        P(None, None, None, "ch", None),
        P("ch"),
        P("ch", "dp", None, "ha", None),
    )
    return jax.shard_map(
        body,
        mesh=mesh,
        in_specs=placed,
        out_specs=(P("ch", "dp", None, "ha", None), P(None, None, None, "ch", None)),
        check_vma=False,
    )
```

```python
import jax
import jax.numpy as jnp
from jax import lax
from jax.sharding import PartitionSpec as P

GROUPS = 32


EPS = 1e-06


def padded_2(x, sides, width):
    for axis, dim in sides:
        count, length = (lax.axis_size(axis), x.shape[dim])
        up = [(i, (i + 1) % count) for i in range(count - 1)]
        down = [(j, i) for i, j in up]
        last = lax.slice_in_dim(x, length - width, length, axis=dim)
        leading = lax.slice_in_dim(x, 0, width, axis=dim)
        before = lax.ppermute(last, axis, up)
        after = lax.ppermute(leading, axis, down)
        x = jnp.concatenate([before, x, after], axis=dim)
    return x


def frame_mask(frame_count, frames):
    position = lax.broadcasted_iota(jnp.int32, (frame_count.shape[0], frames), 1)
    return (position < frame_count[:, None]).astype(jnp.float32)


def moments(values, mask, groups):
    chans, clips, frames, rows, cols = values.shape
    data = values.astype(jnp.float32).reshape(groups, chans // groups, clips, frames, rows * cols)
    first = jnp.einsum("gkbfp,bf->gb", data, mask)
    second = jnp.einsum("gkbfp,bf->gb", data * data, mask)
    return (first, second)


def normalize(values, first, second, count, gain, shift, groups):
    chans, clips, frames, rows, cols = values.shape
    mean = first / count[None, :]
    var = second / count[None, :] - mean * mean
    scale = lax.rsqrt(var + EPS)
    data = values.astype(jnp.float32).reshape(groups, chans // groups, clips, frames, rows * cols)
    normed = (data - mean[:, None, :, None, None]) * scale[:, None, :, None, None]
    normed = normed.reshape(values.shape)
    return normed * gain[:, None, None, None, None] + shift[:, None, None, None, None]


def attend(carry, queries, keys, values, scale):
    top, total, acc = carry
    scores = jnp.einsum("itc,isc->its", queries, keys, preferred_element_type=jnp.float32) * scale
    new_top = jnp.max(scores, axis=2)
    factor = jnp.exp(top - new_top)
    weights = jnp.exp(scores - new_top[..., None])
    total = total * factor + jnp.sum(weights, axis=2)
    acc = acc * factor[..., None] + jnp.einsum(
        "its,isc->itc", weights.astype(jnp.bfloat16), values, preferred_element_type=jnp.float32
    )
    return (new_top, total, acc)


def tap_stack(padded, time_tap, frames, rows, cols):
    windows = []
    for row_tap in range(3):
        for col_tap in range(3):
            windows.append(
                padded[
                    :,
                    :,
                    time_tap : time_tap + frames,
                    row_tap : row_tap + rows,
                    col_tap : col_tap + cols,
                ]
            )
    return jnp.concatenate(windows, axis=0)


def butterfly_sum(table, axes):
    steps = []
    for axis in axes:
        size = lax.axis_size(axis)
        for bit in range(size.bit_length() - 1):
            steps.append((axis, bit, size))
    length = table.shape[0]
    unit = (1 << len(steps)) * 8
    padded = -(-length // unit) * unit
    work = jnp.pad(table, ((0, padded - length), (0, 0)))
    for axis, bit, size in steps:
        side = (lax.axis_index(axis) >> bit) & 1
        halves = work.reshape(2, work.shape[0] // 2, work.shape[1])
        keep = lax.dynamic_index_in_dim(halves, side, keepdims=False)
        send = lax.dynamic_index_in_dim(halves, 1 - side, keepdims=False)
        perm = [(i, i ^ (1 << bit)) for i in range(size)]
        got = lax.ppermute(send.astype(jnp.bfloat16), axis, perm)
        work = keep + got.astype(jnp.float32)
    work = work.astype(jnp.bfloat16)
    for axis, bit, size in reversed(steps):
        side = (lax.axis_index(axis) >> bit) & 1
        perm = [(i, i ^ (1 << bit)) for i in range(size)]
        got = lax.ppermute(work, axis, perm)
        pair = jnp.stack([work, got])
        first = lax.dynamic_index_in_dim(pair, side, keepdims=False)
        second = lax.dynamic_index_in_dim(pair, 1 - side, keepdims=False)
        work = jnp.concatenate([first, second], axis=0)
    return work[:length].astype(jnp.float32)


def body(
    features,
    frame_count,
    norm1_gain,
    norm1_shift,
    qkv_weight,
    qkv_bias,
    out_weight,
    out_bias,
    norm2_gain,
    norm2_shift,
    conv_weight,
    conv_bias,
    cotangent,
):
    chans, clips, frames, rows, cols = features.shape
    groups = GROUPS // lax.axis_size("ch")
    mask = frame_mask(frame_count, frames)
    count = frame_count.astype(jnp.float32) * (chans // groups * rows * lax.axis_size("ha") * cols)
    first, second = moments(features, mask, groups)
    first, second = lax.psum((first, second), "ha")
    normed = normalize(features, first, second, count, norm1_gain, norm1_shift, groups).astype(
        jnp.bfloat16
    )
    by_frame = lax.all_to_all(normed, "ch", split_axis=2, concat_axis=0, tiled=True)
    width = by_frame.shape[0]
    items = clips * by_frame.shape[2]
    tok_rows = rows * cols
    tokens = by_frame.reshape(width, items, tok_rows)
    queries = lax.dot_general(
        tokens, qkv_weight[:, :width], (((0,), (0,)), ((), ())), preferred_element_type=jnp.float32
    )
    queries = (queries + qkv_bias[:width]).astype(jnp.bfloat16)
    scale = width ** (-0.5)
    start_carry = (
        jnp.full((items, tok_rows), -jnp.inf, jnp.float32),
        jnp.zeros((items, tok_rows), jnp.float32),
        jnp.zeros((items, tok_rows, width), jnp.float32),
    )
    pairs = lax.dot_general(
        tokens, qkv_weight[:, width:], (((0,), (0,)), ((), ())), preferred_element_type=jnp.float32
    )
    pairs = (pairs + qkv_bias[width:]).astype(jnp.bfloat16)
    piece = lax.all_gather(pairs, "ha", axis=1, tiled=True)
    top, total, acc = attend(start_carry, queries, piece[..., :width], piece[..., width:], scale)
    attended = (acc / total[..., None]).astype(jnp.bfloat16)
    projected = lax.dot_general(
        out_weight, attended, (((0,), (2,)), ((), ())), preferred_element_type=jnp.float32
    )
    projected = (projected + out_bias[:, None, None]).astype(jnp.bfloat16).reshape(by_frame.shape)
    update = lax.all_to_all(projected, "ch", split_axis=0, concat_axis=2, tiled=True)
    hidden = (features.astype(jnp.float32) + update.astype(jnp.float32)).astype(jnp.bfloat16)
    first, second = moments(hidden, mask, groups)
    first, second = lax.psum((first, second), "ha")
    gated = jax.nn.silu(
        normalize(hidden, first, second, count, norm2_gain, norm2_shift, groups)
    ).astype(jnp.bfloat16)
    with_rows = padded_2(gated, (("ha", 3),), 1)
    padded = jnp.pad(with_rows, ((0, 0), (0, 0), (2, 0), (0, 0), (1, 1)))
    stacks = [tap_stack(padded, time_tap, frames, rows, cols) for time_tap in range(3)]
    amount = chans * lax.axis_size("ch")
    summed = jnp.zeros((amount, clips, frames, rows, cols), jnp.float32)
    for time_tap in range(3):
        part = conv_weight[time_tap].reshape(9 * chans, amount)
        summed = summed + lax.dot_general(
            part, stacks[time_tap], (((0,), (0,)), ((), ())), preferred_element_type=jnp.float32
        )
    summed, stacks = lax.optimization_barrier((summed.astype(jnp.bfloat16), stacks))
    shares = lax.axis_size("ch")
    parts = summed.reshape((shares, amount // shares) + summed.shape[1:])
    parts = lax.all_to_all(parts, "ch", split_axis=0, concat_axis=0, tiled=True)
    conv_out = jnp.sum(parts.astype(jnp.float32), axis=0)
    mixed = mask[None, :, :, None, None] * (
        hidden.astype(jnp.float32) + conv_out + conv_bias[:, None, None, None, None]
    )
    mixed = mixed.astype(jnp.bfloat16)
    masked_cot = cotangent * mask.astype(jnp.bfloat16)[None, :, :, None, None]
    full_width = chans * lax.axis_size("ch")
    carry = jnp.zeros((3, 9 * chans, full_width), jnp.float32)
    copies = jnp.broadcast_to(masked_cot[None], (shares,) + masked_cot.shape)
    piece = lax.all_to_all(copies, "ch", split_axis=0, concat_axis=0, tiled=True)
    piece = piece.reshape((shares * chans,) + masked_cot.shape[1:])
    start = jnp.int32(0)
    for time_tap in range(3):
        part = lax.dot_general(
            stacks[time_tap],
            piece,
            (((1, 2, 3, 4), (1, 2, 3, 4)), ((), ())),
            preferred_element_type=jnp.float32,
        )
        carry = lax.dynamic_update_slice(
            carry, part[None], (jnp.int32(time_tap), jnp.int32(0), start)
        )
    weight_grad = butterfly_sum(carry.reshape(27 * chans, full_width), ("dp", "ha"))
    weight_grad = weight_grad.reshape(3, 3, 3, chans, full_width)
    return (mixed, weight_grad)


def solution(mesh):
    placed = (
        P("ch", "dp", None, "ha", None),
        P("dp"),
        P("ch"),
        P("ch"),
        P(),
        P(),
        P(),
        P(),
        P("ch"),
        P("ch"),
        P(None, None, None, "ch", None),
        P("ch"),
        P("ch", "dp", None, "ha", None),
    )
    return jax.shard_map(
        body,
        mesh=mesh,
        in_specs=placed,
        out_specs=(P("ch", "dp", None, "ha", None), P(None, None, None, "ch", None)),
        check_vma=False,
    )
```

```python
import jax
import jax.numpy as jnp
from jax import lax
from jax.sharding import PartitionSpec as P

GROUPS = 32


EPS = 1e-06


def padded_2(x, sides, width):
    for axis, dim in sides:
        count, length = (lax.axis_size(axis), x.shape[dim])
        up = [(i, (i + 1) % count) for i in range(count - 1)]
        down = [(j, i) for i, j in up]
        last = lax.slice_in_dim(x, length - width, length, axis=dim)
        leading = lax.slice_in_dim(x, 0, width, axis=dim)
        before = lax.ppermute(last, axis, up)
        after = lax.ppermute(leading, axis, down)
        x = jnp.concatenate([before, x, after], axis=dim)
    return x


def frame_mask(frame_count, frames):
    position = lax.broadcasted_iota(jnp.int32, (frame_count.shape[0], frames), 1)
    return (position < frame_count[:, None]).astype(jnp.float32)


def moments(values, mask, groups):
    chans, clips, frames, rows, cols = values.shape
    data = values.astype(jnp.float32).reshape(groups, chans // groups, clips, frames, rows * cols)
    first = jnp.einsum("gkbfp,bf->gb", data, mask)
    second = jnp.einsum("gkbfp,bf->gb", data * data, mask)
    return (first, second)


def normalize(values, first, second, count, gain, shift, groups):
    chans, clips, frames, rows, cols = values.shape
    mean = first / count[None, :]
    var = second / count[None, :] - mean * mean
    scale = lax.rsqrt(var + EPS)
    data = values.astype(jnp.float32).reshape(groups, chans // groups, clips, frames, rows * cols)
    normed = (data - mean[:, None, :, None, None]) * scale[:, None, :, None, None]
    normed = normed.reshape(values.shape)
    return normed * gain[:, None, None, None, None] + shift[:, None, None, None, None]


def attend(carry, queries, keys, values, scale):
    top, total, acc = carry
    scores = jnp.einsum("itc,isc->its", queries, keys, preferred_element_type=jnp.float32) * scale
    new_top = jnp.max(scores, axis=2)
    factor = jnp.exp(top - new_top)
    weights = jnp.exp(scores - new_top[..., None])
    total = total * factor + jnp.sum(weights, axis=2)
    acc = acc * factor[..., None] + jnp.einsum(
        "its,isc->itc", weights.astype(jnp.bfloat16), values, preferred_element_type=jnp.float32
    )
    return (new_top, total, acc)


def tap_stack(padded, time_tap, frames, rows, cols):
    windows = []
    for row_tap in range(3):
        for col_tap in range(3):
            windows.append(
                padded[
                    :,
                    :,
                    time_tap : time_tap + frames,
                    row_tap : row_tap + rows,
                    col_tap : col_tap + cols,
                ]
            )
    return jnp.concatenate(windows, axis=0)


def butterfly_sum(table, axes):
    steps = []
    for axis in axes:
        size = lax.axis_size(axis)
        for bit in range(size.bit_length() - 1):
            steps.append((axis, bit, size))
    length = table.shape[0]
    unit = (1 << len(steps)) * 8
    padded = -(-length // unit) * unit
    work = jnp.pad(table, ((0, padded - length), (0, 0)))
    for axis, bit, size in steps:
        side = (lax.axis_index(axis) >> bit) & 1
        halves = work.reshape(2, work.shape[0] // 2, work.shape[1])
        keep = lax.dynamic_index_in_dim(halves, side, keepdims=False)
        send = lax.dynamic_index_in_dim(halves, 1 - side, keepdims=False)
        perm = [(i, i ^ (1 << bit)) for i in range(size)]
        got = lax.ppermute(send.astype(jnp.bfloat16), axis, perm)
        work = keep + got.astype(jnp.float32)
    work = work.astype(jnp.bfloat16)
    for axis, bit, size in reversed(steps):
        side = (lax.axis_index(axis) >> bit) & 1
        perm = [(i, i ^ (1 << bit)) for i in range(size)]
        got = lax.ppermute(work, axis, perm)
        pair = jnp.stack([work, got])
        first = lax.dynamic_index_in_dim(pair, side, keepdims=False)
        second = lax.dynamic_index_in_dim(pair, 1 - side, keepdims=False)
        work = jnp.concatenate([first, second], axis=0)
    return work[:length].astype(jnp.float32)


def body(
    features,
    frame_count,
    norm1_gain,
    norm1_shift,
    qkv_weight,
    qkv_bias,
    out_weight,
    out_bias,
    norm2_gain,
    norm2_shift,
    conv_weight,
    conv_bias,
    cotangent,
):
    chans, clips, frames, rows, cols = features.shape
    groups = GROUPS // lax.axis_size("ch")
    mask = frame_mask(frame_count, frames)
    count = frame_count.astype(jnp.float32) * (chans // groups * rows * lax.axis_size("ha") * cols)
    first, second = moments(features, mask, groups)
    first, second = lax.psum((first, second), "ha")
    normed = normalize(features, first, second, count, norm1_gain, norm1_shift, groups).astype(
        jnp.bfloat16
    )
    by_frame = lax.all_to_all(normed, "ch", split_axis=2, concat_axis=0, tiled=True)
    width = by_frame.shape[0]
    items = clips * by_frame.shape[2]
    tok_rows = rows * cols
    tokens = by_frame.reshape(width, items, tok_rows)
    queries = lax.dot_general(
        tokens, qkv_weight[:, :width], (((0,), (0,)), ((), ())), preferred_element_type=jnp.float32
    )
    queries = (queries + qkv_bias[:width]).astype(jnp.bfloat16)
    scale = width ** (-0.5)
    start_carry = (
        jnp.full((items, tok_rows), -jnp.inf, jnp.float32),
        jnp.zeros((items, tok_rows), jnp.float32),
        jnp.zeros((items, tok_rows, width), jnp.float32),
    )
    pairs = lax.dot_general(
        tokens, qkv_weight[:, width:], (((0,), (0,)), ((), ())), preferred_element_type=jnp.float32
    )
    pairs = (pairs + qkv_bias[width:]).astype(jnp.bfloat16)
    piece = lax.all_gather(pairs, "ha", axis=1, tiled=True)
    top, total, acc = attend(start_carry, queries, piece[..., :width], piece[..., width:], scale)
    attended = (acc / total[..., None]).astype(jnp.bfloat16)
    projected = lax.dot_general(
        out_weight, attended, (((0,), (2,)), ((), ())), preferred_element_type=jnp.float32
    )
    projected = (projected + out_bias[:, None, None]).astype(jnp.bfloat16).reshape(by_frame.shape)
    update = lax.all_to_all(projected, "ch", split_axis=0, concat_axis=2, tiled=True)
    hidden = (features.astype(jnp.float32) + update.astype(jnp.float32)).astype(jnp.bfloat16)
    first, second = moments(hidden, mask, groups)
    first, second = lax.psum((first, second), "ha")
    gated = jax.nn.silu(
        normalize(hidden, first, second, count, norm2_gain, norm2_shift, groups)
    ).astype(jnp.bfloat16)
    with_rows = padded_2(gated, (("ha", 3),), 1)
    padded = jnp.pad(with_rows, ((0, 0), (0, 0), (2, 0), (0, 0), (1, 1)))
    stacks = [tap_stack(padded, time_tap, frames, rows, cols) for time_tap in range(3)]
    amount = chans * lax.axis_size("ch")
    summed = jnp.zeros((amount, clips, frames, rows, cols), jnp.float32)
    for time_tap in range(3):
        part = conv_weight[time_tap].reshape(9 * chans, amount)
        summed = summed + lax.dot_general(
            part, stacks[time_tap], (((0,), (0,)), ((), ())), preferred_element_type=jnp.float32
        )
    summed, stacks = lax.optimization_barrier((summed.astype(jnp.bfloat16), stacks))
    shares = lax.axis_size("ch")
    parts = summed.reshape((shares, amount // shares) + summed.shape[1:])
    parts = lax.all_to_all(parts, "ch", split_axis=0, concat_axis=0, tiled=True)
    conv_out = jnp.sum(parts.astype(jnp.float32), axis=0)
    mixed = mask[None, :, :, None, None] * (
        hidden.astype(jnp.float32) + conv_out + conv_bias[:, None, None, None, None]
    )
    mixed = mixed.astype(jnp.bfloat16)
    masked_cot = cotangent * mask.astype(jnp.bfloat16)[None, :, :, None, None]
    full_width = chans * lax.axis_size("ch")
    carry = jnp.zeros((3, 9 * chans, full_width), jnp.float32)
    copies = jnp.broadcast_to(masked_cot[None], (shares,) + masked_cot.shape)
    piece = lax.all_to_all(copies, "ch", split_axis=0, concat_axis=0, tiled=True)
    piece = piece.reshape((shares * chans,) + masked_cot.shape[1:])
    start = jnp.int32(0)
    for time_tap in range(3):
        part = lax.dot_general(
            stacks[time_tap],
            piece,
            (((1, 2, 3, 4), (1, 2, 3, 4)), ((), ())),
            preferred_element_type=jnp.float32,
        )
        carry = lax.dynamic_update_slice(
            carry, part[None], (jnp.int32(time_tap), jnp.int32(0), start)
        )
    parts, carry = lax.optimization_barrier((parts, carry))
    weight_grad = butterfly_sum(carry.reshape(27 * chans, full_width), ("dp", "ha"))
    weight_grad = weight_grad.reshape(3, 3, 3, chans, full_width)
    return (mixed, weight_grad)


def solution(mesh):
    placed = (
        P("ch", "dp", None, "ha", None),
        P("dp"),
        P("ch"),
        P("ch"),
        P(),
        P(),
        P(),
        P(),
        P("ch"),
        P("ch"),
        P(None, None, None, "ch", None),
        P("ch"),
        P("ch", "dp", None, "ha", None),
    )
    return jax.shard_map(
        body,
        mesh=mesh,
        in_specs=placed,
        out_specs=(P("ch", "dp", None, "ha", None), P(None, None, None, "ch", None)),
        check_vma=False,
    )
```

```python
import jax
import jax.numpy as jnp
from jax import lax
from jax.sharding import PartitionSpec as P

GROUPS = 32


EPS = 1e-06


def padded_2(x, sides, width):
    for axis, dim in sides:
        count, length = (lax.axis_size(axis), x.shape[dim])
        up = [(i, (i + 1) % count) for i in range(count - 1)]
        down = [(j, i) for i, j in up]
        last = lax.slice_in_dim(x, length - width, length, axis=dim)
        leading = lax.slice_in_dim(x, 0, width, axis=dim)
        before = lax.ppermute(last, axis, up)
        after = lax.ppermute(leading, axis, down)
        x = jnp.concatenate([before, x, after], axis=dim)
    return x


def frame_mask(frame_count, frames):
    position = lax.broadcasted_iota(jnp.int32, (frame_count.shape[0], frames), 1)
    return (position < frame_count[:, None]).astype(jnp.float32)


def moments(values, mask, groups):
    chans, clips, frames, rows, cols = values.shape
    data = values.astype(jnp.float32).reshape(groups, chans // groups, clips, frames, rows * cols)
    first = jnp.einsum("gkbfp,bf->gb", data, mask)
    second = jnp.einsum("gkbfp,bf->gb", data * data, mask)
    return (first, second)


def normalize(values, first, second, count, gain, shift, groups):
    chans, clips, frames, rows, cols = values.shape
    mean = first / count[None, :]
    var = second / count[None, :] - mean * mean
    scale = lax.rsqrt(var + EPS)
    data = values.astype(jnp.float32).reshape(groups, chans // groups, clips, frames, rows * cols)
    normed = (data - mean[:, None, :, None, None]) * scale[:, None, :, None, None]
    normed = normed.reshape(values.shape)
    return normed * gain[:, None, None, None, None] + shift[:, None, None, None, None]


def attend(carry, queries, keys, values, scale):
    top, total, acc = carry
    scores = jnp.einsum("itc,isc->its", queries, keys, preferred_element_type=jnp.float32) * scale
    new_top = jnp.max(scores, axis=2)
    factor = jnp.exp(top - new_top)
    weights = jnp.exp(scores - new_top[..., None])
    total = total * factor + jnp.sum(weights, axis=2)
    acc = acc * factor[..., None] + jnp.einsum(
        "its,isc->itc", weights.astype(jnp.bfloat16), values, preferred_element_type=jnp.float32
    )
    return (new_top, total, acc)


def tap_stack(padded, time_tap, frames, rows, cols):
    windows = []
    for row_tap in range(3):
        for col_tap in range(3):
            windows.append(
                padded[
                    :,
                    :,
                    time_tap : time_tap + frames,
                    row_tap : row_tap + rows,
                    col_tap : col_tap + cols,
                ]
            )
    return jnp.concatenate(windows, axis=0)


def butterfly_sum(table, axes):
    steps = []
    for axis in axes:
        size = lax.axis_size(axis)
        for bit in range(size.bit_length() - 1):
            steps.append((axis, bit, size))
    length = table.shape[0]
    unit = (1 << len(steps)) * 8
    padded = -(-length // unit) * unit
    work = jnp.pad(table, ((0, padded - length), (0, 0)))
    for axis, bit, size in steps:
        side = (lax.axis_index(axis) >> bit) & 1
        halves = work.reshape(2, work.shape[0] // 2, work.shape[1])
        keep = lax.dynamic_index_in_dim(halves, side, keepdims=False)
        send = lax.dynamic_index_in_dim(halves, 1 - side, keepdims=False)
        perm = [(i, i ^ (1 << bit)) for i in range(size)]
        got = lax.ppermute(send.astype(jnp.bfloat16), axis, perm)
        work = keep + got.astype(jnp.float32)
    work = work.astype(jnp.bfloat16)
    for axis, bit, size in reversed(steps):
        side = (lax.axis_index(axis) >> bit) & 1
        perm = [(i, i ^ (1 << bit)) for i in range(size)]
        got = lax.ppermute(work, axis, perm)
        pair = jnp.stack([work, got])
        first = lax.dynamic_index_in_dim(pair, side, keepdims=False)
        second = lax.dynamic_index_in_dim(pair, 1 - side, keepdims=False)
        work = jnp.concatenate([first, second], axis=0)
    return work[:length].astype(jnp.float32)


def doubling_sum(values, axis):
    size = lax.axis_size(axis)
    for bit in range(size.bit_length() - 1):
        perm = [(i, i ^ (1 << bit)) for i in range(size)]
        got = lax.ppermute(values, axis, perm)
        values = tuple(a + b for a, b in zip(values, got))
    return values


def body(
    features,
    frame_count,
    norm1_gain,
    norm1_shift,
    qkv_weight,
    qkv_bias,
    out_weight,
    out_bias,
    norm2_gain,
    norm2_shift,
    conv_weight,
    conv_bias,
    cotangent,
):
    chans, clips, frames, rows, cols = features.shape
    groups = GROUPS // lax.axis_size("ch")
    mask = frame_mask(frame_count, frames)
    count = frame_count.astype(jnp.float32) * (chans // groups * rows * lax.axis_size("ha") * cols)
    first, second = moments(features, mask, groups)
    first, second = doubling_sum((first, second), "ha")
    normed = normalize(features, first, second, count, norm1_gain, norm1_shift, groups).astype(
        jnp.bfloat16
    )
    by_frame = lax.all_to_all(normed, "ch", split_axis=2, concat_axis=0, tiled=True)
    width = by_frame.shape[0]
    items = clips * by_frame.shape[2]
    tok_rows = rows * cols
    tokens = by_frame.reshape(width, items, tok_rows)
    queries = lax.dot_general(
        tokens, qkv_weight[:, :width], (((0,), (0,)), ((), ())), preferred_element_type=jnp.float32
    )
    queries = (queries + qkv_bias[:width]).astype(jnp.bfloat16)
    scale = width ** (-0.5)
    start_carry = (
        jnp.full((items, tok_rows), -jnp.inf, jnp.float32),
        jnp.zeros((items, tok_rows), jnp.float32),
        jnp.zeros((items, tok_rows, width), jnp.float32),
    )
    pairs = lax.dot_general(
        tokens, qkv_weight[:, width:], (((0,), (0,)), ((), ())), preferred_element_type=jnp.float32
    )
    pairs = (pairs + qkv_bias[width:]).astype(jnp.bfloat16)
    piece = lax.all_gather(pairs, "ha", axis=1, tiled=True)
    top, total, acc = attend(start_carry, queries, piece[..., :width], piece[..., width:], scale)
    attended = (acc / total[..., None]).astype(jnp.bfloat16)
    projected = lax.dot_general(
        out_weight, attended, (((0,), (2,)), ((), ())), preferred_element_type=jnp.float32
    )
    projected = (projected + out_bias[:, None, None]).astype(jnp.bfloat16).reshape(by_frame.shape)
    update = lax.all_to_all(projected, "ch", split_axis=0, concat_axis=2, tiled=True)
    hidden = (features.astype(jnp.float32) + update.astype(jnp.float32)).astype(jnp.bfloat16)
    first, second = moments(hidden, mask, groups)
    first, second = doubling_sum((first, second), "ha")
    gated = jax.nn.silu(
        normalize(hidden, first, second, count, norm2_gain, norm2_shift, groups)
    ).astype(jnp.bfloat16)
    with_rows = padded_2(gated, (("ha", 3),), 1)
    padded = jnp.pad(with_rows, ((0, 0), (0, 0), (2, 0), (0, 0), (1, 1)))
    stacks = [tap_stack(padded, time_tap, frames, rows, cols) for time_tap in range(3)]
    amount = chans * lax.axis_size("ch")
    summed = jnp.zeros((amount, clips, frames, rows, cols), jnp.float32)
    for time_tap in range(3):
        part = conv_weight[time_tap].reshape(9 * chans, amount)
        summed = summed + lax.dot_general(
            part, stacks[time_tap], (((0,), (0,)), ((), ())), preferred_element_type=jnp.float32
        )
    summed, stacks = lax.optimization_barrier((summed.astype(jnp.bfloat16), stacks))
    shares = lax.axis_size("ch")
    parts = summed.reshape((shares, amount // shares) + summed.shape[1:])
    parts = lax.all_to_all(parts, "ch", split_axis=0, concat_axis=0, tiled=True)
    conv_out = jnp.sum(parts.astype(jnp.float32), axis=0)
    mixed = mask[None, :, :, None, None] * (
        hidden.astype(jnp.float32) + conv_out + conv_bias[:, None, None, None, None]
    )
    mixed = mixed.astype(jnp.bfloat16)
    masked_cot = cotangent * mask.astype(jnp.bfloat16)[None, :, :, None, None]
    full_width = chans * lax.axis_size("ch")
    carry = jnp.zeros((3, 9 * chans, full_width), jnp.float32)
    copies = jnp.broadcast_to(masked_cot[None], (shares,) + masked_cot.shape)
    piece = lax.all_to_all(copies, "ch", split_axis=0, concat_axis=0, tiled=True)
    piece = piece.reshape((shares * chans,) + masked_cot.shape[1:])
    start = jnp.int32(0)
    for time_tap in range(3):
        part = lax.dot_general(
            stacks[time_tap],
            piece,
            (((1, 2, 3, 4), (1, 2, 3, 4)), ((), ())),
            preferred_element_type=jnp.float32,
        )
        carry = lax.dynamic_update_slice(
            carry, part[None], (jnp.int32(time_tap), jnp.int32(0), start)
        )
    weight_grad = butterfly_sum(carry.reshape(27 * chans, full_width), ("dp", "ha"))
    weight_grad = weight_grad.reshape(3, 3, 3, chans, full_width)
    return (mixed, weight_grad)


def solution(mesh):
    placed = (
        P("ch", "dp", None, "ha", None),
        P("dp"),
        P("ch"),
        P("ch"),
        P(),
        P(),
        P(),
        P(),
        P("ch"),
        P("ch"),
        P(None, None, None, "ch", None),
        P("ch"),
        P("ch", "dp", None, "ha", None),
    )
    return jax.shard_map(
        body,
        mesh=mesh,
        in_specs=placed,
        out_specs=(P("ch", "dp", None, "ha", None), P(None, None, None, "ch", None)),
        check_vma=False,
    )
```
